512 devices in a mesh: req: 64 (over z_lo, x, y), tp: 8 (over z_hi, core).
Axes of the slice: x: 4, y: 8, z: 8 (z_hi: 4, z_lo: 2; z = z_hi * 2 + z_lo), core: 2. Of those that a mesh axis runs over, the one named last changes fastest.
Arguments:
- q_proj: bfloat16 [64, 128, 3072], P('req', None, 'tp'), may hold values from -24 to 24, as said below
- kv_proj: bfloat16 [64, 128, 2, 1024], P('req', None, None, 'tp'), may hold values from -6 to 6
- q_bias: bfloat16 [3072], P('tp'), may hold values from -3 to 3
- kv_bias: bfloat16 [2, 1024], P(None, 'tp'), may hold values from -3 to 3
- prefix_kv: bfloat16 [64, 1024, 2, 1024], P('req', None, None, 'tp'), may hold values from -24 to 24, as said below
- lengths: int32 [64], P('req'), may hold values from 1 to 128, 4096 in all
- group_of: int32 [64], P('req'), may hold values from 0 to 2
- owner: int32 [3], replicated, may hold values from 0 to 63
- positions: int32 [64, 128], P('req'), may hold values from 1024 to 1278, as said below
- residual: bfloat16 [64, 128, 5120], P('req', None, 'tp'), may hold values from -6 to 6
- out_weight: bfloat16 [3072, 5120], P(None, 'tp'), may hold values from -0.109375 to 0.109375
Outputs:
- hidden: bfloat16 [64, 128, 5120], P('req', None, 'tp')
The draws below stay inside these ranges and needn't reach their ends.
Inputs may be any that keep to these rules, and one draw needn't show every extreme that they name: `q_proj`: projected queries; entries stay within the stated bounds. `prefix_kv`: cached keys are already rotated at prefix positions 0 to 1023. Each request's positions are a start of 1024 or more plus the slot index.
All inputs are finite; a program needn't handle non-finite values. No bound on the sum of `lengths` on one device may be relied on, other than what follows from the above.
Results may differ from the reference program's by a relative error of at most 0.006.
Values may be sent and summed in bfloat16 or wider, within the bound.
No kernel may reach another device: no remote copies, remote signals or barrier semaphores. Data moves between devices by JAX's collectives and lax.ppermute only.
A program may use at most 128 MiB of HBM per device.

```python
import math
import jax
import jax.numpy as jnp
import numpy as np
from jax import lax

D = 5120
HD = 128
HQ_DEV = 3
GROUPS = 3
CAP = 128
PREFIX = 1024
KVH = 8
HEADS = 24
N_REQ = 64


def draw_q_proj(key, part):
    base = jnp.clip(jax.random.normal(jax.random.fold_in(key, 1), (N_REQ, CAP, HEADS * HD), jnp.float32), -6.0, 6.0)
    return base.astype(jnp.bfloat16)


def draw_prefix_kv(key, part):
    base = jnp.clip(jax.random.normal(jax.random.fold_in(key, 3), (N_REQ, PREFIX, 2, KVH * HD), jnp.float32), -6.0, 6.0)
    return base.astype(jnp.bfloat16)


def draw_positions(key, part):
    start = jax.random.randint(jax.random.fold_in(key, 5), (N_REQ, 1), PREFIX, PREFIX + CAP)
    start = start.at[0, 0].set(PREFIX + CAP - 1)
    start = start.at[1, 0].set(PREFIX)
    return (start + jnp.arange(CAP)[None, :]).astype(jnp.int32)


def with_ends(values, rng, least, largest):
    place = [jax.random.randint(jax.random.fold_in(rng, axis), (), 0, length) for axis, length in enumerate(values.shape)]
    main_axis = values.shape.index(max(values.shape))
    neighbour = place[:main_axis] + [(place[main_axis] + 1) % values.shape[main_axis]] + place[main_axis + 1:]
    return values.at[tuple(place)].set(least).at[tuple(neighbour)].set(largest)


def level_of(own_key, shape, shards, smallest, top_value):
    def one(position, blocks):
        draws = jax.random.uniform(jax.random.fold_in(jax.random.fold_in(own_key, 6), position), (blocks,), jnp.float32, smallest / len(shards), top_value / len(shards))
        return jnp.repeat(jnp.exp(draws), shape[position] // blocks).reshape((-1,) + (1,) * (len(shape) - position - 1))

    factor_of = one(*shards[0])
    for cut in shards[1:]:
        factor_of = factor_of * one(*cut)
    return factor_of


def length_profile(count, total, most, lean):
    loads = [(1 << 20) // math.isqrt(standing ** lean) + 1 for standing in range(2, count + 1)]
    rest, holding = total - most - (count - 1), [1] * (count - 1)
    while rest > 0:
        candidates = [i for i in range(count - 1) if holding[i] < most]
        whole, budget = sum([loads[i] for i in candidates]), rest
        for i in candidates:
            addition = min(most - holding[i], max(1, budget * loads[i] // whole), rest)
            holding[i] = holding[i] + addition
            rest = rest - addition
    return np.array([most] + holding)


def uneven_parts(key, number_of, total, limit, skew):
    if number_of == 2:
        one = jax.random.randint(key, (), max(1, total - limit), min(limit, total - 1) + 1)
        return jnp.stack([one, total - one])
    sizes = jnp.asarray(length_profile(number_of, total, limit, skew), jnp.int32)
    couples = (number_of - 1) // 2
    source_of, sink = sizes[1:1 + 2 * couples:2], sizes[2:2 + 2 * couples:2]
    room = jnp.minimum(source_of - 1, limit - sink)
    moved = jax.random.randint(jax.random.fold_in(key, 1), (couples,), 0, 1 << 20) % (room + 1)
    sizes = sizes.at[1:1 + 2 * couples:2].set(source_of - moved).at[2:2 + 2 * couples:2].set(sink + moved)
    return sizes[jax.random.permutation(jax.random.fold_in(key, 2), number_of)]


def normal_values(own_key, extent, width, bound, split=(), kind=jnp.bfloat16):
    gain = level_of(own_key, extent, split, -0.22, 0.18) if split else 1.0
    entries = jax.random.normal(own_key, extent, jnp.float32) * width * gain
    return jnp.minimum(jnp.maximum(entries, -bound), bound).astype(kind)


def setup_inputs(seed: int = 0) -> dict:
    arg_keys = jax.random.split(jax.random.key(seed), 12)
    q_proj = draw_q_proj(jax.random.fold_in(arg_keys[11], 71), 0)
    kv_proj = normal_values(arg_keys[1], (N_REQ, CAP, 2, KVH * HD), 1.0, 6.0, ((0, 64), (3, 8)))
    q_bias = normal_values(arg_keys[2], (HEADS * HD,), 0.5, 3.0, ((0, 8),))
    kv_bias = normal_values(arg_keys[3], (2, KVH * HD), 0.5, 3.0, ((1, 8),))
    prefix_kv = draw_prefix_kv(jax.random.fold_in(arg_keys[11], 71), 0)
    lengths = uneven_parts(arg_keys[5], N_REQ, N_REQ * CAP // 2, CAP, 2).astype(jnp.int32)
    group_of = with_ends(jax.random.randint(arg_keys[6], (N_REQ,), 0, GROUPS), jax.random.fold_in(arg_keys[6], 1), 0, GROUPS - 1).astype(jnp.int32)
    owner = jax.random.randint(arg_keys[7], (GROUPS,), 0, N_REQ).astype(jnp.int32)
    positions = draw_positions(jax.random.fold_in(arg_keys[11], 71), 0)
    residual = normal_values(arg_keys[9], (N_REQ, CAP, D), 1.0, 6.0, ((0, 64), (2, 8)))
    out_weight = normal_values(arg_keys[10], (HEADS * HD, D), (HEADS * HD) ** -0.5, 0.109375, ((1, 8),))
    return {"q_proj": q_proj, "kv_proj": kv_proj, "q_bias": q_bias, "kv_bias": kv_bias, "prefix_kv": prefix_kv, "lengths": lengths, "group_of": group_of, "owner": owner, "positions": positions, "residual": residual, "out_weight": out_weight}


def rotate(vectors, places):
    half = HD // 2
    index = jnp.arange(half).astype(jnp.float32)
    freqs = jnp.exp(index * (-2.0 / HD) * math.log(1000000.0))
    angles = places.astype(jnp.float32)[:, None] * freqs[None, :]
    cosine = jnp.concatenate([jnp.cos(angles), jnp.cos(angles)], axis=-1)[:, None, :]
    sine = jnp.concatenate([jnp.sin(angles), jnp.sin(angles)], axis=-1)[:, None, :]
    turned = jnp.concatenate([-vectors[..., half:], vectors[..., :half]], axis=-1)
    return vectors * cosine + turned * sine

def attend(queries, keys, vals, allowed):
    scores = jnp.einsum('rhd,kd->hrk', queries.astype(jnp.float32), keys.astype(jnp.float32)) * (1.0 / math.sqrt(HD))
    scores = jnp.where(allowed[None], scores, -1e+30)
    top = lax.optimization_barrier(jnp.max(scores, axis=-1, keepdims=True))
    weights = jnp.where(allowed[None], jnp.exp(scores - top), 0.0)
    total = lax.optimization_barrier(jnp.sum(weights, axis=-1))
    rounded = weights.astype(jnp.bfloat16)
    mixed = jnp.einsum('hrk,kd->rhd', rounded.astype(jnp.float32), vals.astype(jnp.float32))
    return mixed / jnp.transpose(total)[:, :, None]

def reference(q_proj, kv_proj, q_bias, kv_bias, prefix_kv, lengths, group_of, owner, positions, residual, out_weight):

    def one_request(items):
        q_rows, kv_rows, length, group, places, resid = items
        owner_col = owner[group].astype(jnp.int32)
        slab = lax.dynamic_index_in_dim(prefix_kv, owner_col, 0, keepdims=False).reshape(PREFIX, 2, KVH, HD)
        queries = q_rows.astype(jnp.float32).reshape(CAP, HEADS, HD) + q_bias.astype(jnp.float32).reshape(HEADS, HD)
        queries = rotate(queries, places).astype(jnp.bfloat16)
        pairs = kv_rows.astype(jnp.float32).reshape(CAP, 2, KVH, HD) + kv_bias.astype(jnp.float32).reshape(2, KVH, HD)
        keys = rotate(pairs[:, 0], places).astype(jnp.bfloat16)
        vals = pairs[:, 1].astype(jnp.bfloat16)
        all_keys = jnp.concatenate([slab[:, 0], keys], axis=0)
        all_vals = jnp.concatenate([slab[:, 1], vals], axis=0)
        slots = jnp.arange(CAP).astype(jnp.int32)
        causal = slots[None, :] <= slots[:, None]
        allowed = jnp.concatenate([jnp.ones((CAP, PREFIX), dtype=bool), causal], axis=1)
        heads = []
        for kv_head in range(KVH):
            heads.append(attend(queries[:, kv_head * HQ_DEV:(kv_head + 1) * HQ_DEV], all_keys[:, kv_head], all_vals[:, kv_head], allowed))
        mixed = jnp.concatenate(heads, axis=1)
        mixed = jnp.where((slots < length)[:, None, None], mixed, 0.0).astype(jnp.bfloat16).reshape(CAP, HEADS * HD)
        proj = jnp.dot(mixed, out_weight, preferred_element_type=jnp.float32)
        return (resid.astype(jnp.float32) + proj).astype(jnp.bfloat16)
    return lax.map(one_request, (q_proj, kv_proj, lengths, group_of, positions, residual))
```

```python
import math

import jax
import jax.numpy as jnp
from jax import lax
from jax.sharding import PartitionSpec as P

HD = 128


def rotate(vectors, places):
    half = HD // 2
    index = jnp.arange(half).astype(jnp.float32)
    freqs = jnp.exp(index * (-2.0 / HD) * math.log(1000000.0))
    angles = places.astype(jnp.float32)[:, None] * freqs[None, :]
    cosine = jnp.concatenate([jnp.cos(angles), jnp.cos(angles)], axis=-1)[:, None, :]
    sine = jnp.concatenate([jnp.sin(angles), jnp.sin(angles)], axis=-1)[:, None, :]
    turned = jnp.concatenate([-vectors[..., half:], vectors[..., :half]], axis=-1)
    return vectors * cosine + turned * sine


def fetch_prefix(slab, group, owner):
    columns = lax.axis_size("req")
    piece = slab.shape[0] // columns
    pieces = slab.reshape(columns, piece, 2, HD)
    tag = jnp.broadcast_to(group.astype(slab.dtype), (columns, 1, 2, HD))
    spread = lax.all_to_all(jnp.concatenate([pieces, tag], axis=1), "req", 0, 0, tiled=True)
    groups = spread[:, piece, 0, 0].astype(jnp.int32)
    owned = [
        jnp.swapaxes(lax.dynamic_index_in_dim(spread, owner[g], 0, keepdims=False)[:piece], 0, 1)
        for g in range(owner.shape[0])
    ]
    outgoing = jnp.broadcast_to(owned[0], (columns, 2, piece, HD))
    for g in range(1, owner.shape[0]):
        outgoing = jnp.where((groups == g)[:, None, None, None], owned[g][None], outgoing)
    return lax.all_to_all(outgoing, "req", 0, 0, tiled=True)


def attend_rows(queries, all_keys, all_vals, length, prefix_len):
    count = queries.shape[0]
    slots = jnp.arange(count)
    causal = slots[None, :] <= slots[:, None]
    allowed = jnp.concatenate([jnp.ones((count, prefix_len), dtype=bool), causal], axis=1)
    scores = jnp.einsum("rhd,kd->hrk", queries, all_keys, preferred_element_type=jnp.float32) * (
        1.0 / math.sqrt(HD)
    )
    scores = jnp.where(allowed[None], scores, -1e30)
    top = jnp.max(scores, axis=-1, keepdims=True)
    weights = jnp.where(allowed[None], jnp.exp(scores - top), 0.0)
    total = jnp.sum(weights, axis=-1)
    rounded = weights.astype(jnp.bfloat16)
    mixed = jnp.einsum("hrk,kd->rhd", rounded, all_vals, preferred_element_type=jnp.float32)
    mixed = mixed / jnp.transpose(total)[:, :, None]
    mixed = jnp.where((slots < length)[:, None, None], mixed, 0.0)
    return mixed.astype(jnp.bfloat16)


def body(
    q_proj,
    kv_proj,
    q_bias,
    kv_bias,
    prefix_kv,
    lengths,
    group_of,
    owner,
    positions,
    residual,
    out_weight,
):
    cap = q_proj.shape[1]
    prefix_len = prefix_kv.shape[1]
    length = lengths[0]
    places = positions[0]
    slab = fetch_prefix(prefix_kv[0], group_of[0], owner)
    queries = q_proj[0].astype(jnp.float32).reshape(cap, -1, HD) + q_bias.astype(
        jnp.float32
    ).reshape(-1, HD)
    queries = rotate(queries, places).astype(jnp.bfloat16)
    pairs = kv_proj[0].astype(jnp.float32) + kv_bias.astype(jnp.float32)
    keys = rotate(pairs[:, 0][:, None, :], places)[:, 0].astype(jnp.bfloat16)
    vals = pairs[:, 1].astype(jnp.bfloat16)
    all_keys = jnp.concatenate([slab[:, 0].reshape(prefix_len, HD), keys], axis=0)
    all_vals = jnp.concatenate([slab[:, 1].reshape(prefix_len, HD), vals], axis=0)
    attended = attend_rows(queries, all_keys, all_vals, length, prefix_len)
    attended = attended.reshape(cap, -1)
    whole_heads = lax.all_gather(attended, "tp", axis=1, tiled=True)
    projected = jnp.dot(whole_heads, out_weight, preferred_element_type=jnp.float32)
    hidden = (residual[0].astype(jnp.float32) + projected).astype(jnp.bfloat16)
    return hidden[None]


def solution(mesh):
    in_specs = (
        P("req", None, "tp"),
        P("req", None, None, "tp"),
        P("tp"),
        P(None, "tp"),
        P("req", None, None, "tp"),
        P("req"),
        P("req"),
        P(),
        P("req", None),
        P("req", None, "tp"),
        P(None, "tp"),
    )
    out_specs = P("req", None, "tp")
    return jax.shard_map(body, mesh=mesh, in_specs=in_specs, out_specs=out_specs, check_vma=False)
```

```python
import functools
import math

import jax
import jax.numpy as jnp
from jax import lax
from jax.experimental import pallas as pl
from jax.experimental.pallas import tpu as pltpu
from jax.sharding import PartitionSpec as P

HD = 128
SCALE = 1.0 / math.sqrt(HD)


def rotate(vectors, places):
    half = HD // 2
    index = jnp.arange(half).astype(jnp.float32)
    freqs = jnp.exp(index * (-2.0 / HD) * math.log(1000000.0))
    angles = places.astype(jnp.float32)[:, None] * freqs[None, :]
    cosine = jnp.concatenate([jnp.cos(angles), jnp.cos(angles)], axis=-1)[:, None, :]
    sine = jnp.concatenate([jnp.sin(angles), jnp.sin(angles)], axis=-1)[:, None, :]
    turned = jnp.concatenate([-vectors[..., half:], vectors[..., :half]], axis=-1)
    return vectors * cosine + turned * sine


def tag_kernel(group_ref, slab_ref, out_ref, tag_ref, sems):
    piece = slab_ref.shape[1]
    data = pltpu.make_async_copy(slab_ref, out_ref.at[:, pl.ds(0, piece)], sems.at[0])
    data.start()
    tag_ref[...] = jnp.full(tag_ref.shape, group_ref[0].astype(jnp.float32), jnp.float32).astype(tag_ref.dtype)
    tags = pltpu.make_async_copy(tag_ref, out_ref.at[:, pl.ds(piece, 1)], sems.at[1])
    tags.start()
    data.wait()
    tags.wait()


def tagged(pieces, group):
    columns, piece = pieces.shape[:2]
    return pl.pallas_call(
        tag_kernel,
        out_shape=jax.ShapeDtypeStruct((columns, piece + 1, 2, HD), pieces.dtype),
        in_specs=[pl.BlockSpec(memory_space=pltpu.SMEM), pl.BlockSpec(memory_space=pltpu.HBM)],
        out_specs=pl.BlockSpec(memory_space=pl.ANY),
        scratch_shapes=[pltpu.VMEM((columns, 1, 2, HD), pieces.dtype), pltpu.SemaphoreType.DMA((2,))],
        compiler_params=pltpu.CompilerParams(vmem_limit_bytes=1 << 20),
        name="tag_pieces",
    )(group, pltpu.with_memory_space_constraint(pieces, pltpu.HBM))


def fetch_prefix(slab, group, owner):
    columns = lax.axis_size("req")
    piece = slab.shape[0] // columns
    pieces = slab.reshape(columns, piece, 2, HD)
    spread = lax.all_to_all(tagged(pieces, group), "req", 0, 0, tiled=True)
    groups = spread[:, piece, :, :][:, :, None, :]
    owned = [
        jnp.swapaxes(lax.dynamic_index_in_dim(spread, owner[g], 0, keepdims=False)[:piece], 0, 1)
        for g in range(owner.shape[0])
    ]
    outgoing = jnp.broadcast_to(owned[0], (columns, 2, piece, HD))
    for g in range(1, owner.shape[0]):
        outgoing = jnp.where(groups == g, owned[g][None], outgoing)
    return lax.all_to_all(outgoing, "req", 0, 0, tiled=True)


def attend_kernel(length_ref, q_ref, slab_ref, keys_ref, vals_ref, out_ref):
    heads, count, _ = q_ref.shape
    prefix_len = slab_ref.shape[0] * slab_ref.shape[2]
    over_d = (((1,), (1,)), ((), ()))
    over_k = (((1,), (0,)), ((), ()))
    prefix_keys = slab_ref[:, 0].reshape(prefix_len, HD)
    prefix_vals = slab_ref[:, 1].reshape(prefix_len, HD)
    row = lax.broadcasted_iota(jnp.int32, (count, count), 0)
    causal = lax.broadcasted_iota(jnp.int32, (count, count), 1) <= row
    live = lax.broadcasted_iota(jnp.int32, (count, HD), 0) < length_ref[0]
    for h in range(heads):
        q = q_ref[h]
        far = lax.dot_general(q, prefix_keys, over_d, preferred_element_type=jnp.float32) * SCALE
        near = lax.dot_general(q, keys_ref[...], over_d, preferred_element_type=jnp.float32) * SCALE
        near = jnp.where(causal, near, -1e30)
        top = jnp.maximum(jnp.max(far, axis=-1, keepdims=True), jnp.max(near, axis=-1, keepdims=True))
        far = jnp.exp(far - top)
        near = jnp.where(causal, jnp.exp(near - top), 0.0)
        total = jnp.sum(far, axis=-1, keepdims=True) + jnp.sum(near, axis=-1, keepdims=True)
        mixed = lax.dot_general(far.astype(jnp.bfloat16), prefix_vals, over_k, preferred_element_type=jnp.float32)
        mixed += lax.dot_general(near.astype(jnp.bfloat16), vals_ref[...], over_k, preferred_element_type=jnp.float32)
        mixed = jnp.where(live, mixed / total, 0.0)
        out_ref[:, h * HD : (h + 1) * HD] = mixed.astype(out_ref.dtype)


def attend(length, queries, slab, keys, vals):
    heads, count, _ = queries.shape
    return pl.pallas_call(
        attend_kernel,
        out_shape=jax.ShapeDtypeStruct((count, heads * HD), jnp.bfloat16),
        in_specs=[pl.BlockSpec(memory_space=pltpu.SMEM)] + [pl.BlockSpec(memory_space=pltpu.VMEM)] * 4,
        out_specs=pl.BlockSpec(memory_space=pltpu.VMEM),
        compiler_params=pltpu.CompilerParams(vmem_limit_bytes=12 << 20),
        name="attend",
    )(length, queries, slab, keys, vals)


def project_kernel(parts_ref, weight_ref, resid_ref, out_ref, held_ref, sems):
    parts, _, width = parts_ref.shape
    copies = [
        pltpu.make_async_copy(weight_ref.at[pl.ds(p * width, width)], held_ref.at[p], sems.at[p])
        for p in range(parts)
    ]
    for copy in copies:
        copy.start()
    total = resid_ref[...].astype(jnp.float32)
    for p in range(parts):
        copies[p].wait()
        total += jnp.dot(parts_ref[p], held_ref[p], preferred_element_type=jnp.float32)
    out_ref[...] = total.astype(out_ref.dtype)


def project(parts, weight, resid):
    count, _, width = parts.shape
    return pl.pallas_call(
        project_kernel,
        out_shape=jax.ShapeDtypeStruct(resid.shape, resid.dtype),
        in_specs=[
            pl.BlockSpec(memory_space=pltpu.VMEM),
            pl.BlockSpec(memory_space=pltpu.HBM),
            pl.BlockSpec(memory_space=pltpu.VMEM),
        ],
        out_specs=pl.BlockSpec(memory_space=pltpu.VMEM),
        scratch_shapes=[
            pltpu.VMEM((count, width, weight.shape[1]), weight.dtype),
            pltpu.SemaphoreType.DMA((count,)),
        ],
        compiler_params=pltpu.CompilerParams(vmem_limit_bytes=12 << 20),
        name="project",
    )(parts, pltpu.with_memory_space_constraint(weight, pltpu.HBM), resid)


def body(
    q_proj,
    kv_proj,
    q_bias,
    kv_bias,
    prefix_kv,
    lengths,
    group_of,
    owner,
    positions,
    residual,
    out_weight,
):
    cap = q_proj.shape[1]
    places = positions[0]
    slab = fetch_prefix(prefix_kv[0], group_of, owner)
    queries = q_proj[0].astype(jnp.float32).reshape(cap, -1, HD) + q_bias.astype(
        jnp.float32
    ).reshape(-1, HD)
    queries = jnp.swapaxes(rotate(queries, places).astype(jnp.bfloat16), 0, 1)
    pairs = kv_proj[0].astype(jnp.float32) + kv_bias.astype(jnp.float32)
    keys = rotate(pairs[:, 0][:, None, :], places)[:, 0].astype(jnp.bfloat16)
    vals = pairs[:, 1].astype(jnp.bfloat16)
    attended = attend(lengths, queries, slab, keys, vals)
    parts = lax.all_gather(attended, "tp", axis=0)
    return project(parts, out_weight, residual[0])[None]


def solution(mesh):
    in_specs = (
        P("req", None, "tp"),
        P("req", None, None, "tp"),
        P("tp"),
        P(None, "tp"),
        P("req", None, None, "tp"),
        P("req"),
        P("req"),
        P(),
        P("req", None),
        P("req", None, "tp"),
        P(None, "tp"),
    )
    out_specs = P("req", None, "tp")
    return jax.shard_map(body, mesh=mesh, in_specs=in_specs, out_specs=out_specs, check_vma=False)
```

```python
import functools
import math

import jax
import jax.numpy as jnp
from jax import lax
from jax.experimental import pallas as pl
from jax.experimental.pallas import tpu as pltpu
from jax.sharding import PartitionSpec as P

HD = 128
SCALE = 1.0 / math.sqrt(HD)


def rotate(vectors, places):
    half = HD // 2
    index = jnp.arange(half).astype(jnp.float32)
    freqs = jnp.exp(index * (-2.0 / HD) * math.log(1000000.0))
    angles = places.astype(jnp.float32)[:, None] * freqs[None, :]
    cosine = jnp.concatenate([jnp.cos(angles), jnp.cos(angles)], axis=-1)[:, None, :]
    sine = jnp.concatenate([jnp.sin(angles), jnp.sin(angles)], axis=-1)[:, None, :]
    turned = jnp.concatenate([-vectors[..., half:], vectors[..., :half]], axis=-1)
    return vectors * cosine + turned * sine


def tag_kernel(group_ref, slab_ref, out_ref, sem):
    piece = slab_ref.shape[1]
    data = pltpu.make_async_copy(slab_ref, out_ref.at[:, pl.ds(0, piece)], sem)
    data.start()
    shape = (out_ref.shape[0], 1) + out_ref.shape[2:]
    group = group_ref[0].astype(jnp.float32)
    out_ref[:, piece:] = jnp.full(shape, group, jnp.float32).astype(out_ref.dtype)
    data.wait()


def tagged(pieces, group):
    columns, piece = pieces.shape[:2]
    return pl.pallas_call(
        tag_kernel,
        out_shape=jax.ShapeDtypeStruct((columns, piece + 1, 2, HD), pieces.dtype),
        in_specs=[pl.BlockSpec(memory_space=pltpu.SMEM), pl.BlockSpec(memory_space=pltpu.HBM)],
        out_specs=pl.BlockSpec(memory_space=pltpu.VMEM),
        scratch_shapes=[pltpu.SemaphoreType.DMA],
        compiler_params=pltpu.CompilerParams(vmem_limit_bytes=2 << 20),
        name="tag_pieces",
    )(group, pltpu.with_memory_space_constraint(pieces, pltpu.HBM))


def fetch_prefix(slab, group, owner):
    columns = lax.axis_size("req")
    piece = slab.shape[0] // columns
    pieces = slab.reshape(columns, piece, 2, HD)
    spread = lax.all_to_all(tagged(pieces, group), "req", 0, 0, tiled=True)
    groups = spread[:, piece, :, :][:, :, None, :]
    owned = [
        jnp.swapaxes(lax.dynamic_index_in_dim(spread, owner[g], 0, keepdims=False)[:piece], 0, 1)
        for g in range(owner.shape[0])
    ]
    outgoing = jnp.broadcast_to(owned[0], (columns, 2, piece, HD))
    for g in range(1, owner.shape[0]):
        outgoing = jnp.where(groups == g, owned[g][None], outgoing)
    return lax.all_to_all(outgoing, "req", 0, 0, tiled=True)


def attend_kernel(length_ref, q_ref, slab_ref, keys_ref, vals_ref, out_ref):
    heads, count, _ = q_ref.shape
    prefix_len = slab_ref.shape[0] * slab_ref.shape[2]
    over_d = (((1,), (1,)), ((), ()))
    over_k = (((1,), (0,)), ((), ()))
    prefix_keys = slab_ref[:, 0].reshape(prefix_len, HD)
    prefix_vals = slab_ref[:, 1].reshape(prefix_len, HD)
    row = lax.broadcasted_iota(jnp.int32, (count, count), 0)
    causal = lax.broadcasted_iota(jnp.int32, (count, count), 1) <= row
    live = lax.broadcasted_iota(jnp.int32, (count, HD), 0) < length_ref[0]
    for h in range(heads):
        q = q_ref[h]
        far = lax.dot_general(q, prefix_keys, over_d, preferred_element_type=jnp.float32) * SCALE
        near = lax.dot_general(q, keys_ref[...], over_d, preferred_element_type=jnp.float32) * SCALE
        near = jnp.where(causal, near, -1e30)
        top = jnp.maximum(jnp.max(far, axis=-1, keepdims=True), jnp.max(near, axis=-1, keepdims=True))
        far = jnp.exp(far - top)
        near = jnp.where(causal, jnp.exp(near - top), 0.0)
        total = jnp.sum(far, axis=-1, keepdims=True) + jnp.sum(near, axis=-1, keepdims=True)
        mixed = lax.dot_general(far.astype(jnp.bfloat16), prefix_vals, over_k, preferred_element_type=jnp.float32)
        mixed += lax.dot_general(near.astype(jnp.bfloat16), vals_ref[...], over_k, preferred_element_type=jnp.float32)
        mixed = jnp.where(live, mixed / total, 0.0)
        out_ref[:, h * HD : (h + 1) * HD] = mixed.astype(out_ref.dtype)


def attend(length, queries, slab, keys, vals):
    heads, count, _ = queries.shape
    return pl.pallas_call(
        attend_kernel,
        out_shape=jax.ShapeDtypeStruct((count, heads * HD), jnp.bfloat16),
        in_specs=[pl.BlockSpec(memory_space=pltpu.SMEM)] + [pl.BlockSpec(memory_space=pltpu.VMEM)] * 4,
        out_specs=pl.BlockSpec(memory_space=pltpu.VMEM),
        compiler_params=pltpu.CompilerParams(vmem_limit_bytes=12 << 20),
        name="attend",
    )(length, queries, slab, keys, vals)


HELD = 5


def project_kernel(parts_ref, weight_ref, held_ref, resid_ref, out_ref, late_ref, sems):
    parts, _, width = parts_ref.shape
    late = late_ref.shape[0]
    copies = [
        pltpu.make_async_copy(weight_ref.at[pl.ds(p * width, width)], late_ref.at[p], sems.at[p])
        for p in range(late)
    ]
    for copy in copies:
        copy.start()
    total = resid_ref[...].astype(jnp.float32)
    for p in range(late, parts):
        rows = held_ref[(p - late) * width : (p - late + 1) * width, :]
        total += jnp.dot(parts_ref[p], rows, preferred_element_type=jnp.float32)
    for p in range(late):
        copies[p].wait()
        total += jnp.dot(parts_ref[p], late_ref[p], preferred_element_type=jnp.float32)
    out_ref[...] = total.astype(out_ref.dtype)


def project(parts, weight, resid):
    count, _, width = parts.shape
    late = count - HELD
    return pl.pallas_call(
        project_kernel,
        out_shape=jax.ShapeDtypeStruct(resid.shape, resid.dtype),
        in_specs=[
            pl.BlockSpec(memory_space=pltpu.VMEM),
            pl.BlockSpec(memory_space=pltpu.HBM),
            pl.BlockSpec(memory_space=pltpu.VMEM),
            pl.BlockSpec(memory_space=pltpu.VMEM),
        ],
        out_specs=pl.BlockSpec(memory_space=pltpu.VMEM),
        scratch_shapes=[
            pltpu.VMEM((late, width, weight.shape[1]), weight.dtype),
            pltpu.SemaphoreType.DMA((late,)),
        ],
        compiler_params=pltpu.CompilerParams(vmem_limit_bytes=6 << 20),
        name="project",
    )(parts, pltpu.with_memory_space_constraint(weight, pltpu.HBM), weight[late * width :], resid)


def body(
    q_proj,
    kv_proj,
    q_bias,
    kv_bias,
    prefix_kv,
    lengths,
    group_of,
    owner,
    positions,
    residual,
    out_weight,
):
    cap = q_proj.shape[1]
    places = positions[0]
    slab = fetch_prefix(prefix_kv[0], group_of, owner)
    queries = q_proj[0].astype(jnp.float32).reshape(cap, -1, HD) + q_bias.astype(
        jnp.float32
    ).reshape(-1, HD)
    queries = jnp.swapaxes(rotate(queries, places).astype(jnp.bfloat16), 0, 1)
    pairs = kv_proj[0].astype(jnp.float32) + kv_bias.astype(jnp.float32)
    keys = rotate(pairs[:, 0][:, None, :], places)[:, 0].astype(jnp.bfloat16)
    vals = pairs[:, 1].astype(jnp.bfloat16)
    attended = attend(lengths, queries, slab, keys, vals)
    parts = lax.all_gather(attended, "tp", axis=0)
    return project(parts, out_weight, residual[0])[None]


def solution(mesh):
    in_specs = (
        P("req", None, "tp"),
        P("req", None, None, "tp"),
        P("tp"),
        P(None, "tp"),
        P("req", None, None, "tp"),
        P("req"),
        P("req"),
        P(),
        P("req", None),
        P("req", None, "tp"),
        P(None, "tp"),
    )
    out_specs = P("req", None, "tp")
    return jax.shard_map(body, mesh=mesh, in_specs=in_specs, out_specs=out_specs, check_vma=False)
```

```python
import functools
import math

import jax
import jax.numpy as jnp
from jax import lax
from jax.experimental import pallas as pl
from jax.experimental.pallas import tpu as pltpu
from jax.sharding import PartitionSpec as P

HD = 128
SCALE = 1.0 / math.sqrt(HD)


def turns(places):
    half = HD // 2
    index = jnp.arange(half).astype(jnp.float32)
    freqs = jnp.exp(index * (-2.0 / HD) * math.log(1000000.0))
    angles = places.astype(jnp.float32)[:, None] * freqs[None, :]
    cosine, sine = jnp.cos(angles), jnp.sin(angles)
    return jnp.concatenate([cosine, cosine], axis=-1), jnp.concatenate([-sine, sine], axis=-1)


def prepare_kernel(q_ref, kv_ref, q_bias_ref, kv_bias_ref, cos_ref, sin_ref, q_out, k_out, v_out):
    cosine, sine = cos_ref[...], sin_ref[...]

    def rotated(x):
        return (x * cosine + pltpu.roll(x, HD // 2, 1) * sine).astype(jnp.bfloat16)

    for h in range(q_out.shape[0]):
        x = q_ref[:, h * HD : (h + 1) * HD].astype(jnp.float32)
        q_out[h] = rotated(x + q_bias_ref[h : h + 1].astype(jnp.float32))
    bias = kv_bias_ref[...].astype(jnp.float32)
    k_out[...] = rotated(kv_ref[0].astype(jnp.float32) + bias[0:1])
    v_out[...] = (kv_ref[1].astype(jnp.float32) + bias[1:2]).astype(jnp.bfloat16)


def prepare(q_rows, kv_rows, q_bias, kv_bias, places):
    count = q_rows.shape[0]
    heads = q_rows.shape[1] // HD
    flat = jax.ShapeDtypeStruct((count, HD), jnp.bfloat16)
    return pl.pallas_call(
        prepare_kernel,
        out_shape=(jax.ShapeDtypeStruct((heads, count, HD), jnp.bfloat16), flat, flat),
        in_specs=[pl.BlockSpec(memory_space=pltpu.VMEM)] * 6,
        out_specs=(pl.BlockSpec(memory_space=pltpu.VMEM),) * 3,
        compiler_params=pltpu.CompilerParams(vmem_limit_bytes=4 << 20),
        name="prepare",
    )(q_rows, jnp.swapaxes(kv_rows, 0, 1), q_bias.reshape(heads, HD), kv_bias, *turns(places))


def tag_kernel(group_ref, slab_ref, out_ref, sem):
    piece = slab_ref.shape[1]
    data = pltpu.make_async_copy(slab_ref, out_ref.at[:, pl.ds(0, piece)], sem)
    data.start()
    shape = (out_ref.shape[0], 1) + out_ref.shape[2:]
    group = group_ref[0].astype(jnp.float32)
    out_ref[:, piece:] = jnp.full(shape, group, jnp.float32).astype(out_ref.dtype)
    data.wait()


def tagged(pieces, group):
    columns, piece = pieces.shape[:2]
    return pl.pallas_call(
        tag_kernel,
        out_shape=jax.ShapeDtypeStruct((columns, piece + 1, 2, HD), pieces.dtype),
        in_specs=[pl.BlockSpec(memory_space=pltpu.SMEM), pl.BlockSpec(memory_space=pltpu.HBM)],
        out_specs=pl.BlockSpec(memory_space=pltpu.VMEM),
        scratch_shapes=[pltpu.SemaphoreType.DMA],
        compiler_params=pltpu.CompilerParams(vmem_limit_bytes=2 << 20),
        name="tag_pieces",
    )(group, pltpu.with_memory_space_constraint(pieces, pltpu.HBM))


def choose_kernel(owner_ref, spread_ref, out_ref, held_ref, sems):
    columns, tagged_piece = spread_ref.shape[:2]
    piece = tagged_piece - 1
    owned = []
    for g in range(owner_ref.shape[0]):
        pairs = spread_ref[owner_ref[g], pl.ds(0, piece)].astype(jnp.float32)
        owned.append(jnp.concatenate([pairs[:, 0], pairs[:, 1]], axis=0).astype(out_ref.dtype))
    step = columns // sems.shape[0]
    copies = []
    for c in range(columns):
        tag = jnp.broadcast_to(spread_ref[c, piece, 0:1, :], owned[0].shape)
        chosen = owned[0]
        for g in range(1, len(owned)):
            chosen = jnp.where(tag == float(g), owned[g], chosen)
        held_ref[c] = chosen
        if c % step == step - 1:
            rows = pl.ds(c + 1 - step, step)
            copies.append(pltpu.make_async_copy(held_ref.at[rows], out_ref.at[rows], sems.at[c // step]))
            copies[-1].start()
    for copy in copies:
        copy.wait()


def choose(owner, spread):
    columns, tagged_piece = spread.shape[:2]
    shape = (columns, 2 * (tagged_piece - 1), HD)
    return pl.pallas_call(
        choose_kernel,
        out_shape=jax.ShapeDtypeStruct(shape, spread.dtype),
        in_specs=[pl.BlockSpec(memory_space=pltpu.SMEM), pl.BlockSpec(memory_space=pltpu.VMEM)],
        out_specs=pl.BlockSpec(memory_space=pltpu.HBM),
        scratch_shapes=[pltpu.VMEM(shape, spread.dtype), pltpu.SemaphoreType.DMA((4,))],
        compiler_params=pltpu.CompilerParams(vmem_limit_bytes=4 << 20),
        name="choose_pieces",
    )(owner, spread)


def fetch_prefix(slab, group, owner):
    columns = lax.axis_size("req")
    pieces = slab.reshape(columns, slab.shape[0] // columns, 2, HD)
    spread = lax.all_to_all(tagged(pieces, group), "req", 0, 0, tiled=True)
    return lax.all_to_all(choose(owner, spread), "req", 0, 0, tiled=True)


def attend_kernel(length_ref, q_ref, slab_ref, keys_ref, vals_ref, out_ref):
    heads, count, _ = q_ref.shape
    piece = slab_ref.shape[1] // 2
    prefix_len = slab_ref.shape[0] * piece
    over_d = (((1,), (1,)), ((), ()))
    over_k = (((1,), (0,)), ((), ()))
    prefix_keys = slab_ref[:, :piece].reshape(prefix_len, HD)
    prefix_vals = slab_ref[:, piece:].reshape(prefix_len, HD)
    row = lax.broadcasted_iota(jnp.int32, (count, count), 0)
    causal = lax.broadcasted_iota(jnp.int32, (count, count), 1) <= row
    live = lax.broadcasted_iota(jnp.int32, (count, HD), 0) < length_ref[0]
    for h in range(heads):
        q = q_ref[h]
        far = lax.dot_general(q, prefix_keys, over_d, preferred_element_type=jnp.float32) * SCALE
        near = lax.dot_general(q, keys_ref[...], over_d, preferred_element_type=jnp.float32) * SCALE
        near = jnp.where(causal, near, -1e30)
        top = jnp.maximum(jnp.max(far, axis=-1, keepdims=True), jnp.max(near, axis=-1, keepdims=True))
        far = jnp.exp(far - top)
        near = jnp.where(causal, jnp.exp(near - top), 0.0)
        total = jnp.sum(far, axis=-1, keepdims=True) + jnp.sum(near, axis=-1, keepdims=True)
        mixed = lax.dot_general(far.astype(jnp.bfloat16), prefix_vals, over_k, preferred_element_type=jnp.float32)
        mixed += lax.dot_general(near.astype(jnp.bfloat16), vals_ref[...], over_k, preferred_element_type=jnp.float32)
        mixed = jnp.where(live, mixed / total, 0.0)
        out_ref[:, h * HD : (h + 1) * HD] = mixed.astype(out_ref.dtype)


def attend(length, queries, slab, keys, vals):
    heads, count, _ = queries.shape
    return pl.pallas_call(
        attend_kernel,
        out_shape=jax.ShapeDtypeStruct((count, heads * HD), jnp.bfloat16),
        in_specs=[pl.BlockSpec(memory_space=pltpu.SMEM)] + [pl.BlockSpec(memory_space=pltpu.VMEM)] * 4,
        out_specs=pl.BlockSpec(memory_space=pltpu.VMEM),
        compiler_params=pltpu.CompilerParams(vmem_limit_bytes=12 << 20),
        name="attend",
    )(length, queries, slab, keys, vals)


HELD = 5


def project_kernel(parts_ref, weight_ref, held_ref, resid_ref, out_ref, late_ref, sems):
    parts, _, width = parts_ref.shape
    late = late_ref.shape[0]
    copies = [
        pltpu.make_async_copy(weight_ref.at[pl.ds(p * width, width)], late_ref.at[p], sems.at[p])
        for p in range(late)
    ]
    for copy in copies:
        copy.start()
    total = resid_ref[...].astype(jnp.float32)
    for p in range(late, parts):
        rows = held_ref[(p - late) * width : (p - late + 1) * width, :]
        total += jnp.dot(parts_ref[p], rows, preferred_element_type=jnp.float32)
    for p in range(late):
        copies[p].wait()
        total += jnp.dot(parts_ref[p], late_ref[p], preferred_element_type=jnp.float32)
    out_ref[...] = total.astype(out_ref.dtype)


def project(parts, weight, resid):
    count, _, width = parts.shape
    late = count - HELD
    return pl.pallas_call(
        project_kernel,
        out_shape=jax.ShapeDtypeStruct(resid.shape, resid.dtype),
        in_specs=[
            pl.BlockSpec(memory_space=pltpu.VMEM),
            pl.BlockSpec(memory_space=pltpu.HBM),
            pl.BlockSpec(memory_space=pltpu.VMEM),
            pl.BlockSpec(memory_space=pltpu.VMEM),
        ],
        out_specs=pl.BlockSpec(memory_space=pltpu.VMEM),
        scratch_shapes=[
            pltpu.VMEM((late, width, weight.shape[1]), weight.dtype),
            pltpu.SemaphoreType.DMA((late,)),
        ],
        compiler_params=pltpu.CompilerParams(vmem_limit_bytes=6 << 20),
        name="project",
    )(parts, pltpu.with_memory_space_constraint(weight, pltpu.HBM), weight[late * width :], resid)


def body(
    q_proj,
    kv_proj,
    q_bias,
    kv_bias,
    prefix_kv,
    lengths,
    group_of,
    owner,
    positions,
    residual,
    out_weight,
):
    slab = fetch_prefix(prefix_kv[0], group_of, owner)
    queries, keys, vals = prepare(q_proj[0], kv_proj[0], q_bias, kv_bias, positions[0])
    attended = attend(lengths, queries, slab, keys, vals)
    parts = lax.all_gather(attended, "tp", axis=0)
    return project(parts, out_weight, residual[0])[None]


def solution(mesh):
    in_specs = (
        P("req", None, "tp"),
        P("req", None, None, "tp"),
        P("tp"),
        P(None, "tp"),
        P("req", None, None, "tp"),
        P("req"),
        P("req"),
        P(),
        P("req", None),
        P("req", None, "tp"),
        P(None, "tp"),
    )
    out_specs = P("req", None, "tp")
    return jax.shard_map(body, mesh=mesh, in_specs=in_specs, out_specs=out_specs, check_vma=False)
```

```python
import functools
import math

import jax
import jax.numpy as jnp
from jax import lax
from jax.experimental import pallas as pl
from jax.experimental.pallas import tpu as pltpu
from jax.sharding import Mesh, PartitionSpec as P

HD = 128
ORDER = ("y", "zl", "x")
REQ = ("zl", "x", "y")
SCALE = 1.0 / math.sqrt(HD)


def turns(places):
    half = HD // 2
    index = jnp.arange(half).astype(jnp.float32)
    freqs = jnp.exp(index * (-2.0 / HD) * math.log(1000000.0))
    angles = places.astype(jnp.float32)[:, None] * freqs[None, :]
    cosine, sine = jnp.cos(angles), jnp.sin(angles)
    return jnp.concatenate([cosine, cosine], axis=-1), jnp.concatenate([-sine, sine], axis=-1)


def prepare_kernel(q_ref, kv_ref, q_bias_ref, kv_bias_ref, cos_ref, sin_ref, q_out, k_out, v_out):
    cosine, sine = cos_ref[...], sin_ref[...]

    def rotated(x):
        return (x * cosine + pltpu.roll(x, HD // 2, 1) * sine).astype(jnp.bfloat16)

    for h in range(q_out.shape[0]):
        x = q_ref[:, h * HD : (h + 1) * HD].astype(jnp.float32)
        q_out[h] = rotated(x + q_bias_ref[h : h + 1].astype(jnp.float32))
    bias = kv_bias_ref[...].astype(jnp.float32)
    k_out[...] = rotated(kv_ref[0].astype(jnp.float32) + bias[0:1])
    v_out[...] = (kv_ref[1].astype(jnp.float32) + bias[1:2]).astype(jnp.bfloat16)


def prepare(q_rows, kv_rows, q_bias, kv_bias, places):
    count = q_rows.shape[0]
    heads = q_rows.shape[1] // HD
    flat = jax.ShapeDtypeStruct((count, HD), jnp.bfloat16)
    return pl.pallas_call(
        prepare_kernel,
        out_shape=(jax.ShapeDtypeStruct((heads, count, HD), jnp.bfloat16), flat, flat),
        in_specs=[pl.BlockSpec(memory_space=pltpu.VMEM)] * 6,
        out_specs=(pl.BlockSpec(memory_space=pltpu.VMEM),) * 3,
        compiler_params=pltpu.CompilerParams(vmem_limit_bytes=4 << 20),
        name="prepare",
    )(q_rows, jnp.swapaxes(kv_rows, 0, 1), q_bias.reshape(heads, HD), kv_bias, *turns(places))


def tag_kernel(group_ref, slab_ref, out_ref, sem):
    piece = slab_ref.shape[1]
    data = pltpu.make_async_copy(slab_ref, out_ref.at[:, pl.ds(0, piece)], sem)
    data.start()
    shape = (out_ref.shape[0], 1) + out_ref.shape[2:]
    group = group_ref[0].astype(jnp.float32)
    out_ref[:, piece:] = jnp.full(shape, group, jnp.float32).astype(out_ref.dtype)
    data.wait()


def tagged(pieces, group):
    columns, piece = pieces.shape[:2]
    return pl.pallas_call(
        tag_kernel,
        out_shape=jax.ShapeDtypeStruct((columns, piece + 1, 2, HD), pieces.dtype),
        in_specs=[pl.BlockSpec(memory_space=pltpu.SMEM), pl.BlockSpec(memory_space=pltpu.HBM)],
        out_specs=pl.BlockSpec(memory_space=pltpu.VMEM),
        scratch_shapes=[pltpu.SemaphoreType.DMA],
        compiler_params=pltpu.CompilerParams(vmem_limit_bytes=2 << 20),
        name="tag_pieces",
    )(group, pltpu.with_memory_space_constraint(pieces, pltpu.HBM))


def choose_kernel(owner_ref, spread_ref, out_ref, held_ref, sems):
    columns, tagged_piece = spread_ref.shape[:2]
    piece = tagged_piece - 1
    owned = []
    for g in range(owner_ref.shape[0]):
        pairs = spread_ref[owner_ref[g], pl.ds(0, piece)].astype(jnp.float32)
        owned.append(jnp.concatenate([pairs[:, 0], pairs[:, 1]], axis=0).astype(out_ref.dtype))
    step = columns // sems.shape[0]
    copies = []
    for c in range(columns):
        tag = jnp.broadcast_to(spread_ref[c, piece, 0:1, :], owned[0].shape)
        chosen = owned[0]
        for g in range(1, len(owned)):
            chosen = jnp.where(tag == float(g), owned[g], chosen)
        held_ref[c] = chosen
        if c % step == step - 1:
            rows = pl.ds(c + 1 - step, step)
            copies.append(pltpu.make_async_copy(held_ref.at[rows], out_ref.at[rows], sems.at[c // step]))
            copies[-1].start()
    for copy in copies:
        copy.wait()


def choose(owner, spread):
    columns, tagged_piece = spread.shape[:2]
    shape = (columns, 2 * (tagged_piece - 1), HD)
    return pl.pallas_call(
        choose_kernel,
        out_shape=jax.ShapeDtypeStruct(shape, spread.dtype),
        in_specs=[pl.BlockSpec(memory_space=pltpu.SMEM), pl.BlockSpec(memory_space=pltpu.VMEM)],
        out_specs=pl.BlockSpec(memory_space=pltpu.HBM),
        scratch_shapes=[pltpu.VMEM(shape, spread.dtype), pltpu.SemaphoreType.DMA((4,))],
        compiler_params=pltpu.CompilerParams(vmem_limit_bytes=4 << 20),
        name="choose_pieces",
    )(owner, spread)


def reorder(owner):
    y, x, zl = owner % 8, owner // 8 % 4, owner // 32
    return (y * 2 + zl) * 4 + x


def fetch_prefix(slab, group, owner):
    columns = lax.axis_size(ORDER)
    pieces = slab.reshape(columns, slab.shape[0] // columns, 2, HD)
    owner = reorder(owner)
    outgoing, owner = lax.optimization_barrier((tagged(pieces, group), owner))
    spread = lax.all_to_all(outgoing, ORDER, 0, 0, tiled=True)
    return lax.all_to_all(choose(owner, spread), ORDER, 0, 0, tiled=True)


def attend_kernel(length_ref, q_ref, slab_ref, keys_ref, vals_ref, out_ref):
    heads, count, _ = q_ref.shape
    piece = slab_ref.shape[1] // 2
    prefix_len = slab_ref.shape[0] * piece
    over_d = (((1,), (1,)), ((), ()))
    over_k = (((1,), (0,)), ((), ()))
    prefix_keys = slab_ref[:, :piece].reshape(prefix_len, HD)
    prefix_vals = slab_ref[:, piece:].reshape(prefix_len, HD)
    row = lax.broadcasted_iota(jnp.int32, (count, count), 0)
    causal = lax.broadcasted_iota(jnp.int32, (count, count), 1) <= row
    live = lax.broadcasted_iota(jnp.int32, (count, HD), 0) < length_ref[0]
    for h in range(heads):
        q = q_ref[h]
        far = lax.dot_general(q, prefix_keys, over_d, preferred_element_type=jnp.float32) * SCALE
        near = lax.dot_general(q, keys_ref[...], over_d, preferred_element_type=jnp.float32) * SCALE
        near = jnp.where(causal, near, -1e30)
        top = jnp.maximum(jnp.max(far, axis=-1, keepdims=True), jnp.max(near, axis=-1, keepdims=True))
        far = jnp.exp(far - top)
        near = jnp.where(causal, jnp.exp(near - top), 0.0)
        total = jnp.sum(far, axis=-1, keepdims=True) + jnp.sum(near, axis=-1, keepdims=True)
        mixed = lax.dot_general(far.astype(jnp.bfloat16), prefix_vals, over_k, preferred_element_type=jnp.float32)
        mixed += lax.dot_general(near.astype(jnp.bfloat16), vals_ref[...], over_k, preferred_element_type=jnp.float32)
        mixed = jnp.where(live, mixed / total, 0.0)
        out_ref[:, h * HD : (h + 1) * HD] = mixed.astype(out_ref.dtype)


def attend(length, queries, slab, keys, vals):
    heads, count, _ = queries.shape
    return pl.pallas_call(
        attend_kernel,
        out_shape=jax.ShapeDtypeStruct((count, heads * HD), jnp.bfloat16),
        in_specs=[pl.BlockSpec(memory_space=pltpu.SMEM)] + [pl.BlockSpec(memory_space=pltpu.VMEM)] * 4,
        out_specs=pl.BlockSpec(memory_space=pltpu.VMEM),
        compiler_params=pltpu.CompilerParams(vmem_limit_bytes=12 << 20),
        name="attend",
    )(length, queries, slab, keys, vals)


HELD = 5


def project_kernel(parts_ref, weight_ref, held_ref, resid_ref, out_ref, late_ref, sems):
    parts, _, width = parts_ref.shape
    late = late_ref.shape[0]
    copies = [
        pltpu.make_async_copy(weight_ref.at[pl.ds(p * width, width)], late_ref.at[p], sems.at[p])
        for p in range(late)
    ]
    for copy in copies:
        copy.start()
    total = resid_ref[...].astype(jnp.float32)
    for p in range(late, parts):
        rows = held_ref[(p - late) * width : (p - late + 1) * width, :]
        total += jnp.dot(parts_ref[p], rows, preferred_element_type=jnp.float32)
    for p in range(late):
        copies[p].wait()
        total += jnp.dot(parts_ref[p], late_ref[p], preferred_element_type=jnp.float32)
    out_ref[...] = total.astype(out_ref.dtype)


def project(parts, weight, resid):
    count, _, width = parts.shape
    late = count - HELD
    return pl.pallas_call(
        project_kernel,
        out_shape=jax.ShapeDtypeStruct(resid.shape, resid.dtype),
        in_specs=[
            pl.BlockSpec(memory_space=pltpu.VMEM),
            pl.BlockSpec(memory_space=pltpu.HBM),
            pl.BlockSpec(memory_space=pltpu.VMEM),
            pl.BlockSpec(memory_space=pltpu.VMEM),
        ],
        out_specs=pl.BlockSpec(memory_space=pltpu.VMEM),
        scratch_shapes=[
            pltpu.VMEM((late, width, weight.shape[1]), weight.dtype),
            pltpu.SemaphoreType.DMA((late,)),
        ],
        compiler_params=pltpu.CompilerParams(vmem_limit_bytes=6 << 20),
        name="project",
    )(parts, pltpu.with_memory_space_constraint(weight, pltpu.HBM), weight[late * width :], resid)


def body(
    q_proj,
    kv_proj,
    q_bias,
    kv_bias,
    prefix_kv,
    lengths,
    group_of,
    owner,
    positions,
    residual,
    out_weight,
):
    slab = fetch_prefix(prefix_kv[0], group_of, owner)
    queries, keys, vals = prepare(q_proj[0], kv_proj[0], q_bias, kv_bias, positions[0])
    attended = attend(lengths, queries, slab, keys, vals)
    parts = lax.all_gather(attended, "tp", axis=0)
    return project(parts, out_weight, residual[0])[None]


def solution(mesh):
    mesh = Mesh(mesh.devices.reshape(2, 4, 8, 8), REQ + ("tp",))
    in_specs = (
        P(REQ, None, "tp"),
        P(REQ, None, None, "tp"),
        P("tp"),
        P(None, "tp"),
        P(REQ, None, None, "tp"),
        P(REQ),
        P(REQ),
        P(),
        P(REQ, None),
        P(REQ, None, "tp"),
        P(None, "tp"),
    )
    out_specs = P(REQ, None, "tp")
    return jax.shard_map(body, mesh=mesh, in_specs=in_specs, out_specs=out_specs, check_vma=False)
```

```python
import functools
import math

import jax
import jax.numpy as jnp
from jax import lax
from jax.experimental import pallas as pl
from jax.experimental.pallas import tpu as pltpu
from jax.sharding import Mesh, PartitionSpec as P

HD = 128
ORDER = ("y", "zl", "x")
REQ = ("zl", "x", "y")
SCALE = 1.0 / math.sqrt(HD)


def turns(places):
    half = HD // 2
    index = jnp.arange(half).astype(jnp.float32)
    freqs = jnp.exp(index * (-2.0 / HD) * math.log(1000000.0))
    angles = places.astype(jnp.float32)[:, None] * freqs[None, :]
    cosine, sine = jnp.cos(angles), jnp.sin(angles)
    return jnp.concatenate([cosine, cosine], axis=-1), jnp.concatenate([-sine, sine], axis=-1)


def prepare_kernel(q_ref, kv_ref, q_bias_ref, kv_bias_ref, cos_ref, sin_ref, q_out, k_out, v_out):
    cosine, sine = cos_ref[...], sin_ref[...]

    def rotated(x):
        return (x * cosine + pltpu.roll(x, HD // 2, 1) * sine).astype(jnp.bfloat16)

    for h in range(q_out.shape[0]):
        x = q_ref[:, h * HD : (h + 1) * HD].astype(jnp.float32)
        q_out[h] = rotated(x + q_bias_ref[h : h + 1].astype(jnp.float32))
    bias = kv_bias_ref[...].astype(jnp.float32)
    k_out[...] = rotated(kv_ref[0].astype(jnp.float32) + bias[0:1])
    v_out[...] = (kv_ref[1].astype(jnp.float32) + bias[1:2]).astype(jnp.bfloat16)


def prepare(q_rows, kv_rows, q_bias, kv_bias, places):
    count = q_rows.shape[0]
    heads = q_rows.shape[1] // HD
    flat = jax.ShapeDtypeStruct((count, HD), jnp.bfloat16)
    return pl.pallas_call(
        prepare_kernel,
        out_shape=(jax.ShapeDtypeStruct((heads, count, HD), jnp.bfloat16), flat, flat),
        in_specs=[pl.BlockSpec(memory_space=pltpu.VMEM)] * 6,
        out_specs=(pl.BlockSpec(memory_space=pltpu.VMEM),) * 3,
        compiler_params=pltpu.CompilerParams(vmem_limit_bytes=4 << 20),
        name="prepare",
    )(q_rows, jnp.swapaxes(kv_rows, 0, 1), q_bias.reshape(heads, HD), kv_bias, *turns(places))


def tag_kernel(group_ref, slab_ref, out_ref, sem):
    piece = slab_ref.shape[1]
    data = pltpu.make_async_copy(slab_ref, out_ref.at[:, pl.ds(0, piece)], sem)
    data.start()
    shape = (out_ref.shape[0], 1) + out_ref.shape[2:]
    group = group_ref[0].astype(jnp.float32)
    out_ref[:, piece:] = jnp.full(shape, group, jnp.float32).astype(out_ref.dtype)
    data.wait()


def tagged(pieces, group):
    columns, piece = pieces.shape[:2]
    return pl.pallas_call(
        tag_kernel,
        out_shape=jax.ShapeDtypeStruct((columns, piece + 1, 2, HD), pieces.dtype),
        in_specs=[pl.BlockSpec(memory_space=pltpu.SMEM), pl.BlockSpec(memory_space=pltpu.HBM)],
        out_specs=pl.BlockSpec(memory_space=pltpu.VMEM),
        scratch_shapes=[pltpu.SemaphoreType.DMA],
        compiler_params=pltpu.CompilerParams(vmem_limit_bytes=2 << 20),
        name="tag_pieces",
    )(group, pltpu.with_memory_space_constraint(pieces, pltpu.HBM))


def choose_kernel(owner_ref, spread_ref, out_ref, held_ref, sems):
    columns, tagged_piece = spread_ref.shape[:2]
    piece = tagged_piece - 1
    owned = []
    for g in range(owner_ref.shape[0]):
        pairs = spread_ref[owner_ref[g], pl.ds(0, piece)].astype(jnp.float32)
        owned.append(jnp.concatenate([pairs[:, 0], pairs[:, 1]], axis=0).astype(out_ref.dtype))
    step = columns // sems.shape[0]
    copies = []
    for c in range(columns):
        tag = jnp.broadcast_to(spread_ref[c, piece, 0:1, :], owned[0].shape)
        chosen = owned[0]
        for g in range(1, len(owned)):
            chosen = jnp.where(tag == float(g), owned[g], chosen)
        held_ref[c] = chosen
        if c % step == step - 1:
            rows = pl.ds(c + 1 - step, step)
            copies.append(pltpu.make_async_copy(held_ref.at[rows], out_ref.at[rows], sems.at[c // step]))
            copies[-1].start()
    for copy in copies:
        copy.wait()


def choose(owner, spread):
    columns, tagged_piece = spread.shape[:2]
    shape = (columns, 2 * (tagged_piece - 1), HD)
    return pl.pallas_call(
        choose_kernel,
        out_shape=jax.ShapeDtypeStruct(shape, spread.dtype),
        in_specs=[pl.BlockSpec(memory_space=pltpu.SMEM), pl.BlockSpec(memory_space=pltpu.VMEM)],
        out_specs=pl.BlockSpec(memory_space=pltpu.HBM),
        scratch_shapes=[pltpu.VMEM(shape, spread.dtype), pltpu.SemaphoreType.DMA((4,))],
        compiler_params=pltpu.CompilerParams(vmem_limit_bytes=4 << 20),
        name="choose_pieces",
    )(owner, spread)


def reorder(owner):
    y, x, zl = owner % 8, owner // 8 % 4, owner // 32
    return (y * 2 + zl) * 4 + x


def fetch_prefix(slab, group, owner):
    columns = lax.axis_size(ORDER)
    pieces = slab.reshape(columns, slab.shape[0] // columns, 2, HD)
    owner = reorder(owner)
    outgoing, owner = lax.optimization_barrier((tagged(pieces, group), owner))
    spread = lax.all_to_all(outgoing, ORDER, 0, 0, tiled=True)
    return lax.all_to_all(choose(owner, spread), ORDER, 0, 0, tiled=True)


def attend_kernel(length_ref, q_ref, slab_ref, keys_ref, vals_ref, out_ref):
    heads, count, _ = q_ref.shape
    piece = slab_ref.shape[1] // 2
    prefix_len = slab_ref.shape[0] * piece
    over_d = (((1,), (1,)), ((), ()))
    over_k = (((1,), (0,)), ((), ()))
    prefix_keys = slab_ref[:, :piece].reshape(prefix_len, HD)
    prefix_vals = slab_ref[:, piece:].reshape(prefix_len, HD)
    row = lax.broadcasted_iota(jnp.int32, (count, count), 0)
    causal = lax.broadcasted_iota(jnp.int32, (count, count), 1) <= row
    causal = jnp.concatenate([causal] * heads, axis=0)
    live = lax.broadcasted_iota(jnp.int32, (count, HD), 0) < length_ref[0]
    q = q_ref[...].reshape(heads * count, HD)
    far = lax.dot_general(q, prefix_keys, over_d, preferred_element_type=jnp.float32)
    near = lax.dot_general(q, keys_ref[...], over_d, preferred_element_type=jnp.float32)
    near = jnp.where(causal, near, -1e30)
    top = jnp.maximum(jnp.max(far, axis=-1, keepdims=True), jnp.max(near, axis=-1, keepdims=True))
    far = jnp.exp((far - top) * SCALE)
    near = jnp.where(causal, jnp.exp((near - top) * SCALE), 0.0)
    total = jnp.sum(far, axis=-1, keepdims=True) + jnp.sum(near, axis=-1, keepdims=True)
    mixed = lax.dot_general(far.astype(jnp.bfloat16), prefix_vals, over_k, preferred_element_type=jnp.float32)
    mixed += lax.dot_general(near.astype(jnp.bfloat16), vals_ref[...], over_k, preferred_element_type=jnp.float32)
    mixed = mixed / total
    for h in range(heads):
        rows = mixed[h * count : (h + 1) * count]
        out_ref[:, h * HD : (h + 1) * HD] = jnp.where(live, rows, 0.0).astype(out_ref.dtype)


def attend(length, queries, slab, keys, vals):
    heads, count, _ = queries.shape
    return pl.pallas_call(
        attend_kernel,
        out_shape=jax.ShapeDtypeStruct((count, heads * HD), jnp.bfloat16),
        in_specs=[pl.BlockSpec(memory_space=pltpu.SMEM)] + [pl.BlockSpec(memory_space=pltpu.VMEM)] * 4,
        out_specs=pl.BlockSpec(memory_space=pltpu.VMEM),
        compiler_params=pltpu.CompilerParams(vmem_limit_bytes=12 << 20),
        name="attend",
    )(length, queries, slab, keys, vals)


HELD = 5


def project_kernel(parts_ref, weight_ref, held_ref, resid_ref, out_ref, late_ref, sems):
    parts, _, width = parts_ref.shape
    late = late_ref.shape[0]
    copies = [
        pltpu.make_async_copy(weight_ref.at[pl.ds(p * width, width)], late_ref.at[p], sems.at[p])
        for p in range(late)
    ]
    for copy in copies:
        copy.start()
    total = resid_ref[...].astype(jnp.float32)
    for p in range(late, parts):
        rows = held_ref[(p - late) * width : (p - late + 1) * width, :]
        total += jnp.dot(parts_ref[p], rows, preferred_element_type=jnp.float32)
    for p in range(late):
        copies[p].wait()
        total += jnp.dot(parts_ref[p], late_ref[p], preferred_element_type=jnp.float32)
    out_ref[...] = total.astype(out_ref.dtype)


def project(parts, weight, resid):
    count, _, width = parts.shape
    late = count - HELD
    return pl.pallas_call(
        project_kernel,
        out_shape=jax.ShapeDtypeStruct(resid.shape, resid.dtype),
        in_specs=[
            pl.BlockSpec(memory_space=pltpu.VMEM),
            pl.BlockSpec(memory_space=pltpu.HBM),
            pl.BlockSpec(memory_space=pltpu.VMEM),
            pl.BlockSpec(memory_space=pltpu.VMEM),
        ],
        out_specs=pl.BlockSpec(memory_space=pltpu.VMEM),
        scratch_shapes=[
            pltpu.VMEM((late, width, weight.shape[1]), weight.dtype),
            pltpu.SemaphoreType.DMA((late,)),
        ],
        compiler_params=pltpu.CompilerParams(vmem_limit_bytes=6 << 20),
        name="project",
    )(parts, pltpu.with_memory_space_constraint(weight, pltpu.HBM), weight[late * width :], resid)


def body(
    q_proj,
    kv_proj,
    q_bias,
    kv_bias,
    prefix_kv,
    lengths,
    group_of,
    owner,
    positions,
    residual,
    out_weight,
):
    slab = fetch_prefix(prefix_kv[0], group_of, owner)
    queries, keys, vals = prepare(q_proj[0], kv_proj[0], q_bias, kv_bias, positions[0])
    attended = attend(lengths, queries, slab, keys, vals)
    parts = lax.all_gather(attended, "tp", axis=0)
    return project(parts, out_weight, residual[0])[None]


def solution(mesh):
    mesh = Mesh(mesh.devices.reshape(2, 4, 8, 8), REQ + ("tp",))
    in_specs = (
        P(REQ, None, "tp"),
        P(REQ, None, None, "tp"),
        P("tp"),
        P(None, "tp"),
        P(REQ, None, None, "tp"),
        P(REQ),
        P(REQ),
        P(),
        P(REQ, None),
        P(REQ, None, "tp"),
        P(None, "tp"),
    )
    out_specs = P(REQ, None, "tp")
    return jax.shard_map(body, mesh=mesh, in_specs=in_specs, out_specs=out_specs, check_vma=False)
```

```python
import functools
import math

import jax
import jax.numpy as jnp
from jax import lax
from jax.experimental import pallas as pl
from jax.experimental.pallas import tpu as pltpu
from jax.sharding import Mesh, PartitionSpec as P

HD = 128
ORDER = ("y", "zl", "x")
REQ = ("zl", "x", "y")
SCALE = 1.0 / math.sqrt(HD)


def turns(places):
    half = HD // 2
    index = jnp.arange(half).astype(jnp.float32)
    freqs = jnp.exp(index * (-2.0 / HD) * math.log(1000000.0))
    angles = places.astype(jnp.float32)[:, None] * freqs[None, :]
    cosine, sine = jnp.cos(angles), jnp.sin(angles)
    return jnp.concatenate([cosine, cosine], axis=-1), jnp.concatenate([-sine, sine], axis=-1)


def prepare_kernel(q_ref, kv_ref, q_bias_ref, kv_bias_ref, cos_ref, sin_ref, q_out, k_out, v_out):
    cosine, sine = cos_ref[...], sin_ref[...]

    def rotated(x):
        return (x * cosine + pltpu.roll(x, HD // 2, 1) * sine).astype(jnp.bfloat16)

    for h in range(q_out.shape[0]):
        x = q_ref[:, h * HD : (h + 1) * HD].astype(jnp.float32)
        q_out[h] = rotated(x + q_bias_ref[h : h + 1].astype(jnp.float32))
    bias = kv_bias_ref[...].astype(jnp.float32)
    k_out[...] = rotated(kv_ref[0].astype(jnp.float32) + bias[0:1])
    v_out[...] = (kv_ref[1].astype(jnp.float32) + bias[1:2]).astype(jnp.bfloat16)


def prepare(q_rows, kv_rows, q_bias, kv_bias, places):
    count = q_rows.shape[0]
    heads = q_rows.shape[1] // HD
    flat = jax.ShapeDtypeStruct((count, HD), jnp.bfloat16)
    return pl.pallas_call(
        prepare_kernel,
        out_shape=(jax.ShapeDtypeStruct((heads, count, HD), jnp.bfloat16), flat, flat),
        in_specs=[pl.BlockSpec(memory_space=pltpu.VMEM)] * 6,
        out_specs=(pl.BlockSpec(memory_space=pltpu.VMEM),) * 3,
        compiler_params=pltpu.CompilerParams(vmem_limit_bytes=4 << 20),
        name="prepare",
    )(q_rows, jnp.swapaxes(kv_rows, 0, 1), q_bias.reshape(heads, HD), kv_bias, *turns(places))


def tag_kernel(group_ref, slab_ref, out_ref, sem):
    piece = slab_ref.shape[1]
    data = pltpu.make_async_copy(slab_ref, out_ref.at[:, pl.ds(0, piece)], sem)
    data.start()
    shape = (out_ref.shape[0], 1) + out_ref.shape[2:]
    group = group_ref[0].astype(jnp.float32)
    out_ref[:, piece:] = jnp.full(shape, group, jnp.float32).astype(out_ref.dtype)
    data.wait()


def tagged(pieces, group):
    columns, piece = pieces.shape[:2]
    return pl.pallas_call(
        tag_kernel,
        out_shape=jax.ShapeDtypeStruct((columns, piece + 1, 2, HD), pieces.dtype),
        in_specs=[pl.BlockSpec(memory_space=pltpu.SMEM), pl.BlockSpec(memory_space=pltpu.HBM)],
        out_specs=pl.BlockSpec(memory_space=pltpu.VMEM),
        scratch_shapes=[pltpu.SemaphoreType.DMA],
        compiler_params=pltpu.CompilerParams(vmem_limit_bytes=2 << 20),
        name="tag_pieces",
    )(group, pltpu.with_memory_space_constraint(pieces, pltpu.HBM))


def choose_kernel(owner_ref, spread_ref, out_ref, held_ref, sems):
    columns, tagged_piece = spread_ref.shape[:2]
    piece = tagged_piece - 1
    owned = []
    for g in range(owner_ref.shape[0]):
        pairs = spread_ref[owner_ref[g], pl.ds(0, piece)].astype(jnp.float32)
        owned.append(jnp.concatenate([pairs[:, 0], pairs[:, 1]], axis=0).astype(out_ref.dtype))
    step = columns // sems.shape[0]
    copies = []
    for c in range(columns):
        tag = jnp.broadcast_to(spread_ref[c, piece, 0:1, :], owned[0].shape)
        chosen = owned[0]
        for g in range(1, len(owned)):
            chosen = jnp.where(tag == float(g), owned[g], chosen)
        held_ref[c] = chosen
        if c % step == step - 1:
            rows = pl.ds(c + 1 - step, step)
            copies.append(pltpu.make_async_copy(held_ref.at[rows], out_ref.at[rows], sems.at[c // step]))
            copies[-1].start()
    for copy in copies:
        copy.wait()


def choose(owner, spread):
    columns, tagged_piece = spread.shape[:2]
    shape = (columns, 2 * (tagged_piece - 1), HD)
    return pl.pallas_call(
        choose_kernel,
        out_shape=jax.ShapeDtypeStruct(shape, spread.dtype),
        in_specs=[pl.BlockSpec(memory_space=pltpu.SMEM), pl.BlockSpec(memory_space=pltpu.VMEM)],
        out_specs=pl.BlockSpec(memory_space=pltpu.HBM),
        scratch_shapes=[pltpu.VMEM(shape, spread.dtype), pltpu.SemaphoreType.DMA((8,))],
        compiler_params=pltpu.CompilerParams(vmem_limit_bytes=4 << 20),
        name="choose_pieces",
    )(owner, spread)


def reorder(owner):
    y, x, zl = owner % 8, owner // 8 % 4, owner // 32
    return (y * 2 + zl) * 4 + x


def fetch_prefix(slab, group, owner):
    columns = lax.axis_size(ORDER)
    pieces = slab.reshape(columns, slab.shape[0] // columns, 2, HD)
    owner = reorder(owner)
    outgoing, owner = lax.optimization_barrier((tagged(pieces, group), owner))
    spread = lax.all_to_all(outgoing, ORDER, 0, 0, tiled=True)
    return lax.all_to_all(choose(owner, spread), ORDER, 0, 0, tiled=True)


def attend_kernel(length_ref, q_ref, slab_ref, keys_ref, vals_ref, out_ref):
    heads, count, _ = q_ref.shape
    piece = slab_ref.shape[1] // 2
    prefix_len = slab_ref.shape[0] * piece
    over_d = (((1,), (1,)), ((), ()))
    over_k = (((1,), (0,)), ((), ()))
    prefix_keys = slab_ref[:, :piece].reshape(prefix_len, HD)
    prefix_vals = slab_ref[:, piece:].reshape(prefix_len, HD)
    row = lax.broadcasted_iota(jnp.int32, (count, count), 0)
    causal = lax.broadcasted_iota(jnp.int32, (count, count), 1) <= row
    causal = jnp.concatenate([causal] * heads, axis=0)
    live = lax.broadcasted_iota(jnp.int32, (count, HD), 0) < length_ref[0]
    q = q_ref[...].reshape(heads * count, HD)
    far = lax.dot_general(q, prefix_keys, over_d, preferred_element_type=jnp.float32)
    near = lax.dot_general(q, keys_ref[...], over_d, preferred_element_type=jnp.float32)
    near = jnp.where(causal, near, -1e30)
    top = jnp.maximum(jnp.max(far, axis=-1, keepdims=True), jnp.max(near, axis=-1, keepdims=True))
    far = jnp.exp((far - top) * SCALE)
    near = jnp.where(causal, jnp.exp((near - top) * SCALE), 0.0)
    total = jnp.sum(far, axis=-1, keepdims=True) + jnp.sum(near, axis=-1, keepdims=True)
    mixed = lax.dot_general(far.astype(jnp.bfloat16), prefix_vals, over_k, preferred_element_type=jnp.float32)
    mixed += lax.dot_general(near.astype(jnp.bfloat16), vals_ref[...], over_k, preferred_element_type=jnp.float32)
    mixed = mixed / total
    for h in range(heads):
        rows = mixed[h * count : (h + 1) * count]
        out_ref[:, h * HD : (h + 1) * HD] = jnp.where(live, rows, 0.0).astype(out_ref.dtype)


def attend(length, queries, slab, keys, vals):
    heads, count, _ = queries.shape
    return pl.pallas_call(
        attend_kernel,
        out_shape=jax.ShapeDtypeStruct((count, heads * HD), jnp.bfloat16),
        in_specs=[pl.BlockSpec(memory_space=pltpu.SMEM)] + [pl.BlockSpec(memory_space=pltpu.VMEM)] * 4,
        out_specs=pl.BlockSpec(memory_space=pltpu.VMEM),
        compiler_params=pltpu.CompilerParams(vmem_limit_bytes=12 << 20),
        name="attend",
    )(length, queries, slab, keys, vals)


HELD = 5


def project_kernel(parts_ref, weight_ref, held_ref, resid_ref, out_ref, late_ref, sems):
    parts, _, width = parts_ref.shape
    late = late_ref.shape[0]
    copies = [
        pltpu.make_async_copy(weight_ref.at[pl.ds(p * width, width)], late_ref.at[p], sems.at[p])
        for p in range(late)
    ]
    for copy in copies:
        copy.start()
    total = resid_ref[...].astype(jnp.float32)
    for p in range(late, parts):
        rows = held_ref[(p - late) * width : (p - late + 1) * width, :]
        total += jnp.dot(parts_ref[p], rows, preferred_element_type=jnp.float32)
    for p in range(late):
        copies[p].wait()
        total += jnp.dot(parts_ref[p], late_ref[p], preferred_element_type=jnp.float32)
    out_ref[...] = total.astype(out_ref.dtype)


def project(parts, weight, resid):
    count, _, width = parts.shape
    late = count - HELD
    return pl.pallas_call(
        project_kernel,
        out_shape=jax.ShapeDtypeStruct(resid.shape, resid.dtype),
        in_specs=[
            pl.BlockSpec(memory_space=pltpu.VMEM),
            pl.BlockSpec(memory_space=pltpu.HBM),
            pl.BlockSpec(memory_space=pltpu.VMEM),
            pl.BlockSpec(memory_space=pltpu.VMEM),
        ],
        out_specs=pl.BlockSpec(memory_space=pltpu.VMEM),
        scratch_shapes=[
            pltpu.VMEM((late, width, weight.shape[1]), weight.dtype),
            pltpu.SemaphoreType.DMA((late,)),
        ],
        compiler_params=pltpu.CompilerParams(vmem_limit_bytes=6 << 20),
        name="project",
    )(parts, pltpu.with_memory_space_constraint(weight, pltpu.HBM), weight[late * width :], resid)


def body(
    q_proj,
    kv_proj,
    q_bias,
    kv_bias,
    prefix_kv,
    lengths,
    group_of,
    owner,
    positions,
    residual,
    out_weight,
):
    slab = fetch_prefix(prefix_kv[0], group_of, owner)
    queries, keys, vals = prepare(q_proj[0], kv_proj[0], q_bias, kv_bias, positions[0])
    attended = attend(lengths, queries, slab, keys, vals)
    parts = lax.all_gather(attended, "tp", axis=0)
    return project(parts, out_weight, residual[0])[None]


def solution(mesh):
    mesh = Mesh(mesh.devices.reshape(2, 4, 8, 8), REQ + ("tp",))
    in_specs = (
        P(REQ, None, "tp"),
        P(REQ, None, None, "tp"),
        P("tp"),
        P(None, "tp"),
        P(REQ, None, None, "tp"),
        P(REQ),
        P(REQ),
        P(),
        P(REQ, None),
        P(REQ, None, "tp"),
        P(None, "tp"),
    )
    out_specs = P(REQ, None, "tp")
    return jax.shard_map(body, mesh=mesh, in_specs=in_specs, out_specs=out_specs, check_vma=False)
```
